32 devices in a mesh: groups: 2 (over y), hist: 2 (over x), rows: 4 (over z), cols: 2 (over core).
Axes of the slice: x: 2, y: 2, z: 4, core: 2. Of those that a mesh axis runs over, the one named last changes fastest.
Arguments:
- hists: float32 [2, 1024, 4096], P('hist', ('groups', 'rows'), 'cols'), parts along dimension 1, may hold values from 0.2 to 2000, as said below
- log_scaling_fields: float32 [2, 1024, 4096], P('hist', ('groups', 'rows'), 'cols'), parts along dimension 1, may hold values from -1 to 1
- histogram_weight_list: float32 [2], replicated, may hold values from 0.25 to 4
Outputs:
- barycenter: float32 [1024, 4096], P(('groups', 'rows'), 'cols'), parts along dimension 0
- new_logs: float32 [2, 1024, 4096], P('hist', ('groups', 'rows'), 'cols'), parts along dimension 1
The draws below stay inside these ranges and needn't reach their ends.
There are 2 independent parts, one for each index of `groups`. The reference program is written for one: setup_inputs(seed, part) draws one part's arguments, and reference() takes and returns one part's arrays. A program takes and returns all parts, laid end to end along the dimension named above; an argument that names none is the same for every part. Nothing has to cross between parts.
Inputs may be any that keep to these rules, and one draw needn't show every extreme that they name: `hists`: every entry is positive.
All inputs are finite; a program needn't handle non-finite values.
Results may differ from the reference program's by a relative error of at most 0.00021.
Values sent between devices are 32-bit elements; how exact they have to be, the bound alone decides.
A program may use at most 64 MiB of HBM per device.

```python
import math
import jax
import jax.numpy as jnp
from jax import lax

HALF = 32
NHIST = 2
HEIGHT = 512
WIDTH = 4096


def draw_hists(key, part):
    row_key = jax.random.fold_in(key, 11)
    col_key = jax.random.fold_in(key, 12)
    cell_key = jax.random.fold_in(key, 13)
    row_index = jnp.arange(HEIGHT).astype(jnp.float32) / float(max(HEIGHT - 1, 1))
    row_random = jnp.exp(jax.random.uniform(row_key, (HEIGHT,), jnp.float32) * math.log(4.0))
    row_trend = jnp.exp(row_index * math.log(3.0))
    col_scale = jnp.exp(jax.random.uniform(col_key, (WIDTH,), jnp.float32) * math.log(10.0))
    rough_cells = jnp.exp(jax.random.uniform(cell_key, (NHIST, HEIGHT, WIDTH), jnp.float32, -1.0, 1.0))
    row_scale = row_trend * row_random
    return (rough_cells * row_scale[None, :, None] * col_scale[None, None, :]).astype(jnp.float32)


def draw_log_scaling_fields(key, part):
    term_total = 8
    wave_key = jax.random.fold_in(key, 21)
    angle_key = jax.random.fold_in(key, 22)
    phase_key = jax.random.fold_in(key, 23)
    rough_key = jax.random.fold_in(key, 24)
    wave_lengths = 32.0 * jnp.exp(jax.random.uniform(wave_key, (NHIST, term_total), jnp.float32) * math.log(16.0))
    angle_draws = jax.random.uniform(angle_key, (NHIST, term_total), jnp.float32, 0.0, 2.0 * math.pi)
    phase_draws = jax.random.uniform(phase_key, (NHIST, term_total), jnp.float32, 0.0, 2.0 * math.pi)
    row_at = jnp.arange(HEIGHT).astype(jnp.float32)[None, :, None]
    col_at = jnp.arange(WIDTH).astype(jnp.float32)[None, None, :]
    smooth_sum = jnp.zeros((NHIST, HEIGHT, WIDTH), jnp.float32)
    for term_index in range(term_total):
        freq_here = 2.0 * math.pi / wave_lengths[:, term_index]
        freq_rows = (freq_here * jnp.cos(angle_draws[:, term_index]))[:, None, None]
        freq_cols = (freq_here * jnp.sin(angle_draws[:, term_index]))[:, None, None]
        smooth_sum = smooth_sum + jnp.cos(freq_rows * row_at + freq_cols * col_at + phase_draws[:, term_index][:, None, None])
    rough_part = jax.random.uniform(rough_key, (NHIST, HEIGHT, WIDTH), jnp.float32, -1.0, 1.0)
    inner = 0.45 * smooth_sum + 0.15 * rough_part
    return (0.98 * jnp.tanh(inner)).astype(jnp.float32)


def setup_inputs(seed: int = 0, part: int = 0) -> dict:
    key_list = jax.random.split(jax.random.key(seed), 4)
    part_splits = jax.random.split(jax.random.fold_in(key_list[3], part), 4)
    hists = draw_hists(jax.random.fold_in(jax.random.fold_in(key_list[3], part), 71), part)
    log_scaling_fields = draw_log_scaling_fields(jax.random.fold_in(jax.random.fold_in(key_list[3], part), 71), part)
    histogram_weight_list = jnp.clip(jnp.exp(jax.random.uniform(key_list[2], (NHIST,), jnp.float32, math.log(0.25), math.log(4.0))), 0.25, 4.0)
    return dict(hists=hists, log_scaling_fields=log_scaling_fields, histogram_weight_list=histogram_weight_list)


kernel_sigma = 16.0


def kernel_profile():
    offsets = jnp.arange(-HALF, HALF + 1).astype(jnp.float32)
    raw_taps = jnp.exp(-offsets * offsets / (2.0 * kernel_sigma * kernel_sigma))
    return raw_taps / jnp.sum(raw_taps)


def blurred_field(fields):
    stacked = fields[:, None]
    profile = kernel_profile()
    across = lax.conv_general_dilated(stacked, profile.reshape(1, 1, 1, -1), (1, 1), ((0, 0), (HALF, HALF)), precision=lax.Precision.HIGHEST)
    vertical = lax.conv_general_dilated(across, profile.reshape(1, 1, -1, 1), (1, 1), ((HALF, HALF), (0, 0)), precision=lax.Precision.HIGHEST)
    return vertical[:, 0]


def reference(hists, log_scaling_fields, histogram_weight_list):
    scaling_fields = jnp.exp(log_scaling_fields)
    blurred_vertical = blurred_field(scaling_fields)
    ratios = hists / blurred_vertical
    smooth_u = blurred_field(ratios)
    log_blurred = jnp.log(smooth_u)
    log_portions = log_scaling_fields + log_blurred
    lambdas = histogram_weight_list / jnp.sum(histogram_weight_list)
    log_mean = jnp.sum(lambdas[:, None, None] * log_portions, axis=0)
    mean_field = jnp.exp(log_mean)
    total_mass = jnp.sum(mean_field)
    barycenter = mean_field * (HEIGHT * WIDTH / total_mass)
    new_logs = jnp.log(barycenter)[None] - log_blurred
    return (barycenter, new_logs)
```

```python
import functools
import math

import jax
import jax.numpy as jnp
from jax import lax
from jax.experimental import pallas as pl
from jax.experimental.pallas import tpu as pltpu
from jax.sharding import PartitionSpec as P

HALF = 32
SIGMA = 16.0
PIECE = 256
EDGE = 128
MESH = pl.DeviceIdType.MESH
F32 = jnp.float32
BF16 = jnp.bfloat16

TAP_TOTAL = sum(math.exp(-t * t / (2.0 * SIGMA * SIGMA)) for t in range(-HALF, HALF + 1))


def split(x):
    hi = x.astype(BF16)
    lo = (x - hi.astype(F32)).astype(BF16)
    return hi, lo


def dot(a, b):
    return jnp.dot(a, b, preferred_element_type=F32)


def taps(shape, shift):
    a = lax.broadcasted_iota(jnp.int32, shape, 0)
    b = lax.broadcasted_iota(jnp.int32, shape, 1)
    t = (b - a - shift).astype(F32)
    entries = jnp.exp(-t * t / (2.0 * SIGMA * SIGMA)) / TAP_TOTAL
    return jnp.where(jnp.abs(t) <= HALF, entries, 0.0)


def kernel(
    sizes,
    w_ref, v_ref, h_ref,
    mean_ref, diff_ref, scale_ref,
    ev, eh, g1h, g1l, g3h, g3l, r1h, r1l, ch, cl, logs, slots, mass, mslots,
    z_send, z_recv, e_send, e_recv, c_send, c_recv, l_sem, x_send, x_recv, m_send, m_recv,
):
    R, C, H = sizes
    height, width = v_ref.shape
    pieces = width // PIECE
    top = 2 * HALF
    row, col, hist = lax.axis_index("rows"), lax.axis_index("cols"), lax.axis_index("hist")
    flat = row * C + col

    barrier = pltpu.get_barrier_semaphore()
    for k in range(1, R * C):
        other = lax.rem(flat + k, R * C)
        pl.semaphore_signal(
            barrier, inc=1, device_id={"rows": other // C, "cols": lax.rem(other, C)}, device_id_type=MESH
        )
    for k in range(1, H):
        pl.semaphore_signal(barrier, inc=1, device_id={"hist": lax.rem(hist + k, H)}, device_id_type=MESH)

    def own(p):
        cols = pl.ds(pl.multiple_of(p * PIECE, PIECE), PIECE)
        return (
            pltpu.make_async_copy(v_ref.at[:, cols], ev.at[p + 1, pl.ds(top, height)], l_sem.at[0, p]),
            pltpu.make_async_copy(h_ref.at[:, cols], eh.at[p + 1, pl.ds(HALF, height)], l_sem.at[1, p]),
        )

    for p in range(pieces):
        for copy in own(p):
            copy.start()

    pl.semaphore_wait(barrier, R * C - 1 + H - 1)

    def rim(src, dst, depth, edge_rows, send, recv, dev, p, to_up):
        cols = pl.ds(pl.multiple_of(p * PIECE, PIECE), PIECE)
        s = pl.ds(0, depth) if to_up else pl.ds(height - depth, depth)
        d = pl.ds(depth + height, depth) if to_up else pl.ds(0, depth)
        return pltpu.make_async_remote_copy(
            src_ref=src.at[s, cols], dst_ref=dst.at[p + 1, d], send_sem=send, recv_sem=recv,
            device_id=dev, device_id_type=MESH,
        )

    def rims(p, to_up):
        dev = {"rows": row - 1 if to_up else row + 1}
        i = 0 if to_up else 2
        return (
            rim(v_ref, ev, top, None, z_send.at[i, p], z_recv.at[i, p], dev, p, to_up),
            rim(h_ref, eh, HALF, None, z_send.at[i + 1, p], z_recv.at[i + 1, p], dev, p, to_up),
        )

    def side(to_left, up):
        out = []
        scol = pl.ds(0, EDGE) if to_left else pl.ds(width - EDGE, EDGE)
        slot = pieces + 1 if to_left else 0
        dcol = pl.ds(0, EDGE) if to_left else pl.ds(PIECE - EDGE, EDGE)
        dcolumn = col - 1 if to_left else col + 1
        for i, (src, dst, depth) in enumerate(((v_ref, ev, top), (h_ref, eh, HALF))):
            if up == 0:
                s, d = pl.ds(0, height), pl.ds(depth, height)
                dev = {"cols": dcolumn}
                a, b = e_send.at[i, int(to_left)], e_recv.at[i, int(to_left)]
            else:
                s = pl.ds(0, depth) if up < 0 else pl.ds(height - depth, depth)
                d = pl.ds(depth + height, depth) if up < 0 else pl.ds(0, depth)
                dev = {"rows": row + up, "cols": dcolumn}
                n = int(to_left) * 2 + (0 if up < 0 else 1)
                a, b = c_send.at[i, n], c_recv.at[i, n]
            out.append(
                pltpu.make_async_remote_copy(
                    src_ref=src.at[s, scol], dst_ref=dst.at[slot, d, dcol], send_sem=a, recv_sem=b,
                    device_id=dev, device_id_type=MESH,
                )
            )
        return out

    has = {-1: row > 0, 1: row < R - 1}
    has_col = {True: col > 0, False: col < C - 1}

    for up in (-1, 1, 0):
        for to_left in (True, False):
            cond = has_col[to_left]
            if up:
                cond = jnp.logical_and(cond, has[up])

            @pl.when(cond)
            def _():
                for copy in side(to_left, up):
                    copy.start()

    for p in range(pieces):
        for up in (-1, 1):

            @pl.when(has[up])
            def _():
                for copy in rims(p, up < 0):
                    copy.start()

    band = taps(r1h.shape, HALF)
    r1h[...], r1l[...] = split(band)
    for half in range(2):
        rows_in = lax.broadcasted_iota(jnp.int32, (PIECE, PIECE), 0) + half * PIECE
        cols_out = lax.broadcasted_iota(jnp.int32, (PIECE, PIECE), 1)
        t = (rows_in - cols_out - PIECE // 2).astype(F32)
        entries = jnp.exp(-t * t / (2.0 * SIGMA * SIGMA)) / TAP_TOTAL
        ch[half*PIECE:(half+1)*PIECE], cl[half*PIECE:(half+1)*PIECE] = split(jnp.where(jnp.abs(t) <= HALF, entries, 0.0))

    weight_sum = w_ref[0]
    for k in range(1, H):
        weight_sum = weight_sum + w_ref[k]
    own_weight = jnp.full((1, PIECE), w_ref[hist], F32) / jnp.full((1, PIECE), weight_sum, F32)

    def row_ok(rows_count, margin):
        r = lax.broadcasted_iota(jnp.int32, (rows_count, 1), 0) + (row * height - margin)
        return jnp.logical_and(r >= 0, r < R * height)

    def rows_pass(mh, ml, xh, xl):
        return dot(mh[...], xh) + dot(ml[...], xh) + dot(mh[...], xl)

    def scalings_piece(index):
        lanes = lax.broadcasted_iota(jnp.int32, (1, PIECE), 1) + (index - 1) * PIECE
        near = jnp.logical_and(lanes >= -EDGE, lanes < width + EDGE)
        g = lanes + col * width
        ok_cols = jnp.logical_and(near, jnp.logical_and(g >= 0, g < C * width))
        ok = jnp.logical_and(row_ok(height + 2 * top, top), ok_cols)
        f = jnp.where(ok, jnp.exp(ev[index]), 0.0)
        fh, fl = split(f)
        g1h[index], g1l[index] = split(rows_pass(r1h, r1l, fh, fl))

    def cols_pass(ah, al, j):
        xh = jnp.concatenate([ah[j], ah[j + 1]], axis=1)
        xl = jnp.concatenate([al[j], al[j + 1]], axis=1)
        total = dot(xh, ch[...]) + dot(xl, ch[...]) + dot(xh, cl[...])
        return total

    def arrive(conds, make):
        cond = conds[0]
        for c in conds[1:]:
            cond = jnp.logical_and(cond, c)

        @pl.when(cond)
        def _():
            for copy in make():
                copy.wait_recv()

    def wait_side(to_left):
        came = has_col[not to_left]
        arrive((came,), lambda: side(to_left, 0))
        for up in (-1, 1):
            arrive((came, has[-up]), lambda: side(to_left, up))

    wait_side(False)
    scalings_piece(0)

    def x_copy(c, k):
        other = lax.rem(hist + k, H)
        return pltpu.make_async_remote_copy(
            src_ref=slots.at[hist, c], dst_ref=slots.at[hist, c],
            send_sem=x_send.at[k - 1, c], recv_sem=x_recv.at[hist, c],
            device_id={"hist": other}, device_id_type=MESH,
        )

    def step(j, carry):
        @pl.when(j < pieces)
        def _():
            for copy in own(j):
                copy.wait()
            for up in (-1, 1):
                arrive((has[-up],), lambda: rims(j, up < 0))

        @pl.when(j == pieces)
        def _():
            wait_side(True)

        scalings_piece(j + 1)
        smooth_v = cols_pass(g1h, g1l, j)
        masses = jnp.concatenate([eh[j, :, PIECE // 2 :], eh[j + 1, :, : PIECE // 2]], axis=1)
        lanes = lax.broadcasted_iota(jnp.int32, (1, PIECE), 1) + (j * PIECE - PIECE // 2 + col * width)
        ok = jnp.logical_and(
            row_ok(height + top, HALF), jnp.logical_and(lanes >= 0, lanes < C * width)
        )
        ratios = jnp.where(ok, masses / smooth_v, 0.0)
        fill = jnp.zeros((top, PIECE), F32)
        rh, rl = split(jnp.concatenate([ratios, fill], axis=0))
        g3h[j], g3l[j] = split(rows_pass(r1h.at[pl.ds(0, height)], r1l.at[pl.ds(0, height)], rh, rl))

        @pl.when(j >= 1)
        def _():
            c = j - 1
            log_smooth = jnp.log(cols_pass(g3h, g3l, c))
            logs[c] = log_smooth
            slots[hist, c] = own_weight * (ev[c + 1, pl.ds(top, height)] + log_smooth)
            for k in range(1, H):
                x_copy(c, k).start()

        return carry

    for j in range(pieces + 1):
        step(j, 0)

    mass[...] = jnp.zeros_like(mass)

    def combine(c, carry):
        for k in range(1, H):
            source = lax.rem(hist + k, H)
            pltpu.make_async_remote_copy(
                src_ref=slots.at[source, c], dst_ref=slots.at[source, c],
                send_sem=x_send.at[k - 1, c], recv_sem=x_recv.at[source, c],
                device_id={"hist": source}, device_id_type=MESH,
            ).wait_recv()
        log_mean = slots[0, c]
        for k in range(1, H):
            log_mean = log_mean + slots[k, c]
        mean = jnp.exp(log_mean)
        cols = pl.ds(pl.multiple_of(c * PIECE, PIECE), PIECE)
        mean_ref[:, cols] = mean
        diff_ref[:, cols] = log_mean - logs[c]
        part = jnp.sum(mean.reshape(height // 8, 8, PIECE), axis=0)
        mass[...] += part[:, :128] + part[:, 128:]
        return carry

    lax.fori_loop(0, pieces, combine, 0)

    def m_copy(k, index):
        other = lax.rem(flat + k, R * C)
        return pltpu.make_async_remote_copy(
            src_ref=mass, dst_ref=mslots.at[index], send_sem=m_send.at[k - 1], recv_sem=m_recv.at[index],
            device_id={"rows": other // C, "cols": lax.rem(other, C)}, device_id_type=MESH,
        )

    for k in range(1, R * C):
        m_copy(k, flat).start()
    mslots[flat] = mass[...]
    for k in range(1, R * C):
        m_copy(k, lax.rem(flat + k, R * C)).wait_recv()
    total = mslots[0]
    for k in range(1, R * C):
        total = total + mslots[k]
    total = jnp.sum(jnp.sum(total, axis=0, keepdims=True), axis=1, keepdims=True)
    cells = float(height * R * width * C)
    scale_ref[...] = jnp.broadcast_to(cells / total, scale_ref.shape)

    for k in range(1, R * C):
        m_copy(k, flat).wait_send()
    for up in (-1, 1, 0):
        for to_left in (True, False):
            cond = has_col[to_left]
            if up:
                cond = jnp.logical_and(cond, has[up])

            @pl.when(cond)
            def _():
                for copy in side(to_left, up):
                    copy.wait_send()

    def drain(p, carry):
        for up in (-1, 1):

            @pl.when(has[up])
            def _():
                for copy in rims(p, up < 0):
                    copy.wait_send()

        for k in range(1, H):
            x_copy(p, k).wait_send()
        return carry

    lax.fori_loop(0, pieces, drain, 0)


def body(mesh, hists, log_scaling_fields, histogram_weight_list):
    R, C, H = (mesh.shape[a] for a in ("rows", "cols", "hist"))
    masses, fields = hists[0], log_scaling_fields[0]
    height, width = masses.shape
    pieces = width // PIECE
    top = 2 * HALF
    dma = pltpu.SemaphoreType.DMA
    tile = jax.ShapeDtypeStruct((height, width), F32)
    any_spec = pl.BlockSpec(memory_space=pl.ANY)
    vmem = pl.BlockSpec(memory_space=pltpu.VMEM)
    mean, diff, scale = pl.pallas_call(
        functools.partial(kernel, (R, C, H)),
        out_shape=(tile, tile, jax.ShapeDtypeStruct((8, 128), F32)),
        in_specs=[pl.BlockSpec(memory_space=pltpu.SMEM), any_spec, any_spec],
        out_specs=(vmem, vmem, vmem),
        scratch_shapes=[
            pltpu.VMEM((pieces + 2, height + 2 * top, PIECE), F32),
            pltpu.VMEM((pieces + 2, height + top, PIECE), F32),
            pltpu.VMEM((pieces + 2, height + top, PIECE), BF16),
            pltpu.VMEM((pieces + 2, height + top, PIECE), BF16),
            pltpu.VMEM((pieces + 1, height, PIECE), BF16),
            pltpu.VMEM((pieces + 1, height, PIECE), BF16),
            pltpu.VMEM((height + top, height + 2 * top), BF16),
            pltpu.VMEM((height + top, height + 2 * top), BF16),
            pltpu.VMEM((2 * PIECE, PIECE), BF16),
            pltpu.VMEM((2 * PIECE, PIECE), BF16),
            pltpu.VMEM((pieces, height, PIECE), F32),
            pltpu.VMEM((H, pieces, height, PIECE), F32),
            pltpu.VMEM((8, 128), F32),
            pltpu.VMEM((R * C, 8, 128), F32),
            dma((4, pieces)), dma((4, pieces)),
            dma((2, 2)), dma((2, 2)),
            dma((2, 4)), dma((2, 4)),
            dma((2, pieces)),
            dma((max(H - 1, 1), pieces)), dma((H, pieces)),
            dma((max(R * C - 1, 1),)), dma((R * C,)),
        ],
        compiler_params=pltpu.CompilerParams(collective_id=0, has_side_effects=True),
    )(histogram_weight_list, fields, masses)
    factor = scale[0, 0]
    return mean * factor, (diff + jnp.log(factor))[None]


def solution(mesh):
    return jax.shard_map(
        functools.partial(body, mesh),
        mesh=mesh,
        in_specs=(
            P("hist", ("groups", "rows"), "cols"),
            P("hist", ("groups", "rows"), "cols"),
            P(),
        ),
        out_specs=(P(("groups", "rows"), "cols"), P("hist", ("groups", "rows"), "cols")),
        check_vma=False,
    )
```

```python
import functools
import math

import jax
import jax.numpy as jnp
from jax import lax
from jax.experimental import pallas as pl
from jax.experimental.pallas import tpu as pltpu
from jax.sharding import PartitionSpec as P

HALF = 32
SIGMA = 16.0
PIECE = 256
EDGE = 128
MESH = pl.DeviceIdType.MESH
F32 = jnp.float32
BF16 = jnp.bfloat16

TAP_TOTAL = sum(math.exp(-t * t / (2.0 * SIGMA * SIGMA)) for t in range(-HALF, HALF + 1))


def split(x):
    hi = x.astype(BF16)
    lo = (x - hi.astype(F32)).astype(BF16)
    return hi, lo


def dot(a, b):
    return jnp.dot(a, b, preferred_element_type=F32)


def taps(shape, shift):
    a = lax.broadcasted_iota(jnp.int32, shape, 0)
    b = lax.broadcasted_iota(jnp.int32, shape, 1)
    t = (b - a - shift).astype(F32)
    entries = jnp.exp(-t * t / (2.0 * SIGMA * SIGMA)) / TAP_TOTAL
    return jnp.where(jnp.abs(t) <= HALF, entries, 0.0)


def kernel(
    sizes,
    w_ref, v_ref, h_ref,
    mean_ref, diff_ref, scale_ref,
    ev, eh, g1h, g1l, g3h, g3l, r1h, r1l, ch, cl, logs, slots, mass, mslots,
    z_send, z_recv, e_send, e_recv, c_send, c_recv, l_sem, x_send, x_recv, m_send, m_recv,
):
    R, C, H = sizes
    height, width = v_ref.shape
    pieces = width // PIECE
    top = 2 * HALF
    row, col, hist = lax.axis_index("rows"), lax.axis_index("cols"), lax.axis_index("hist")
    flat = row * C + col

    barrier = pltpu.get_barrier_semaphore()
    for k in range(1, R * C):
        other = lax.rem(flat + k, R * C)
        pl.semaphore_signal(
            barrier, inc=1, device_id={"rows": other // C, "cols": lax.rem(other, C)}, device_id_type=MESH
        )
    for k in range(1, H):
        pl.semaphore_signal(barrier, inc=1, device_id={"hist": lax.rem(hist + k, H)}, device_id_type=MESH)

    def own(p):
        cols = pl.ds(pl.multiple_of(p * PIECE, PIECE), PIECE)
        return (
            pltpu.make_async_copy(v_ref.at[:, cols], ev.at[p + 1, pl.ds(top, height)], l_sem.at[0, p]),
            pltpu.make_async_copy(h_ref.at[:, cols], eh.at[p + 1, pl.ds(HALF, height)], l_sem.at[1, p]),
        )

    for p in range(pieces):
        for copy in own(p):
            copy.start()

    pl.semaphore_wait(barrier, R * C - 1 + H - 1)

    def rim(src, dst, depth, edge_rows, send, recv, dev, p, to_up):
        cols = pl.ds(pl.multiple_of(p * PIECE, PIECE), PIECE)
        s = pl.ds(0, depth) if to_up else pl.ds(height - depth, depth)
        d = pl.ds(depth + height, depth) if to_up else pl.ds(0, depth)
        return pltpu.make_async_remote_copy(
            src_ref=src.at[s, cols], dst_ref=dst.at[p + 1, d], send_sem=send, recv_sem=recv,
            device_id=dev, device_id_type=MESH,
        )

    def rims(p, to_up):
        dev = {"rows": row - 1 if to_up else row + 1}
        i = 0 if to_up else 2
        return (
            rim(v_ref, ev, top, None, z_send.at[i, p], z_recv.at[i, p], dev, p, to_up),
            rim(h_ref, eh, HALF, None, z_send.at[i + 1, p], z_recv.at[i + 1, p], dev, p, to_up),
        )

    def side(to_left, up):
        out = []
        scol = pl.ds(0, EDGE) if to_left else pl.ds(width - EDGE, EDGE)
        slot = pieces + 1 if to_left else 0
        dcol = pl.ds(0, EDGE) if to_left else pl.ds(PIECE - EDGE, EDGE)
        dcolumn = col - 1 if to_left else col + 1
        for i, (src, dst, depth) in enumerate(((v_ref, ev, top), (h_ref, eh, HALF))):
            if up == 0:
                s, d = pl.ds(0, height), pl.ds(depth, height)
                dev = {"cols": dcolumn}
                a, b = e_send.at[i, int(to_left)], e_recv.at[i, int(to_left)]
            else:
                s = pl.ds(0, depth) if up < 0 else pl.ds(height - depth, depth)
                d = pl.ds(depth + height, depth) if up < 0 else pl.ds(0, depth)
                dev = {"rows": row + up, "cols": dcolumn}
                n = int(to_left) * 2 + (0 if up < 0 else 1)
                a, b = c_send.at[i, n], c_recv.at[i, n]
            out.append(
                pltpu.make_async_remote_copy(
                    src_ref=src.at[s, scol], dst_ref=dst.at[slot, d, dcol], send_sem=a, recv_sem=b,
                    device_id=dev, device_id_type=MESH,
                )
            )
        return out

    has = {-1: row > 0, 1: row < R - 1}
    has_col = {True: col > 0, False: col < C - 1}

    def send_sides(to_left):
        for up in (-1, 1, 0):
            cond = has_col[to_left]
            if up:
                cond = jnp.logical_and(cond, has[up])

            @pl.when(cond)
            def _():
                for copy in side(to_left, up):
                    copy.start()

    send_sides(False)
    for p in range(pieces):
        for up in (-1, 1):

            @pl.when(has[up])
            def _():
                for copy in rims(p, up < 0):
                    copy.start()

    send_sides(True)

    band = taps(r1h.shape, HALF)
    r1h[...], r1l[...] = split(band)
    for half in range(2):
        rows_in = lax.broadcasted_iota(jnp.int32, (PIECE, PIECE), 0) + half * PIECE
        cols_out = lax.broadcasted_iota(jnp.int32, (PIECE, PIECE), 1)
        t = (rows_in - cols_out - PIECE // 2).astype(F32)
        entries = jnp.exp(-t * t / (2.0 * SIGMA * SIGMA)) / TAP_TOTAL
        ch[half*PIECE:(half+1)*PIECE], cl[half*PIECE:(half+1)*PIECE] = split(jnp.where(jnp.abs(t) <= HALF, entries, 0.0))

    weight_sum = w_ref[0]
    for k in range(1, H):
        weight_sum = weight_sum + w_ref[k]
    own_weight = jnp.full((1, PIECE), w_ref[hist], F32) / jnp.full((1, PIECE), weight_sum, F32)

    def row_ok(rows_count, margin):
        r = lax.broadcasted_iota(jnp.int32, (rows_count, 1), 0) + (row * height - margin)
        return jnp.logical_and(r >= 0, r < R * height)

    def rows_pass(mh, ml, xh, xl):
        return dot(mh[...], xh) + dot(ml[...], xh) + dot(mh[...], xl)

    def scalings_piece(index):
        lanes = lax.broadcasted_iota(jnp.int32, (1, PIECE), 1) + (index - 1) * PIECE
        near = jnp.logical_and(lanes >= -EDGE, lanes < width + EDGE)
        g = lanes + col * width
        ok_cols = jnp.logical_and(near, jnp.logical_and(g >= 0, g < C * width))
        ok = jnp.logical_and(row_ok(height + 2 * top, top), ok_cols)
        f = jnp.where(ok, jnp.exp(ev[index]), 0.0)
        fh, fl = split(f)
        g1h[index], g1l[index] = split(rows_pass(r1h, r1l, fh, fl))

    def cols_pass(ah, al, j):
        xh = jnp.concatenate([ah[j], ah[j + 1]], axis=1)
        xl = jnp.concatenate([al[j], al[j + 1]], axis=1)
        total = dot(xh, ch[...]) + dot(xl, ch[...]) + dot(xh, cl[...])
        return total

    def arrive(conds, make):
        cond = conds[0]
        for c in conds[1:]:
            cond = jnp.logical_and(cond, c)

        @pl.when(cond)
        def _():
            for copy in make():
                copy.wait_recv()

    def wait_side(to_left):
        came = has_col[not to_left]
        arrive((came,), lambda: side(to_left, 0))
        for up in (-1, 1):
            arrive((came, has[-up]), lambda: side(to_left, up))

    wait_side(False)
    scalings_piece(0)

    def x_copy(c, k):
        other = lax.rem(hist + k, H)
        return pltpu.make_async_remote_copy(
            src_ref=slots.at[hist, c], dst_ref=slots.at[hist, c],
            send_sem=x_send.at[k - 1, c], recv_sem=x_recv.at[hist, c],
            device_id={"hist": other}, device_id_type=MESH,
        )

    def step(j, carry):
        @pl.when(j < pieces)
        def _():
            for copy in own(j):
                copy.wait()
            for up in (-1, 1):
                arrive((has[-up],), lambda: rims(j, up < 0))

        @pl.when(j == pieces)
        def _():
            wait_side(True)

        scalings_piece(j + 1)
        smooth_v = cols_pass(g1h, g1l, j)
        masses = jnp.concatenate([eh[j, :, PIECE // 2 :], eh[j + 1, :, : PIECE // 2]], axis=1)
        lanes = lax.broadcasted_iota(jnp.int32, (1, PIECE), 1) + (j * PIECE - PIECE // 2 + col * width)
        ok = jnp.logical_and(
            row_ok(height + top, HALF), jnp.logical_and(lanes >= 0, lanes < C * width)
        )
        ratios = jnp.where(ok, masses / smooth_v, 0.0)
        fill = jnp.zeros((top, PIECE), F32)
        rh, rl = split(jnp.concatenate([ratios, fill], axis=0))
        g3h[j], g3l[j] = split(rows_pass(r1h.at[pl.ds(0, height)], r1l.at[pl.ds(0, height)], rh, rl))

        @pl.when(j >= 1)
        def _():
            c = j - 1
            log_smooth = jnp.log(cols_pass(g3h, g3l, c))
            logs[c] = log_smooth
            slots[hist, c] = own_weight * (ev[c + 1, pl.ds(top, height)] + log_smooth)
            for k in range(1, H):
                x_copy(c, k).start()

        return carry

    for j in range(pieces + 1):
        step(j, 0)

    mass[...] = jnp.zeros_like(mass)

    def combine(c, carry):
        for k in range(1, H):
            source = lax.rem(hist + k, H)
            pltpu.make_async_remote_copy(
                src_ref=slots.at[source, c], dst_ref=slots.at[source, c],
                send_sem=x_send.at[k - 1, c], recv_sem=x_recv.at[source, c],
                device_id={"hist": source}, device_id_type=MESH,
            ).wait_recv()
        log_mean = slots[0, c]
        for k in range(1, H):
            log_mean = log_mean + slots[k, c]
        mean = jnp.exp(log_mean)
        cols = pl.ds(pl.multiple_of(c * PIECE, PIECE), PIECE)
        mean_ref[:, cols] = mean
        diff_ref[:, cols] = log_mean - logs[c]
        part = jnp.sum(mean.reshape(height // 8, 8, PIECE), axis=0)
        mass[...] += part[:, :128] + part[:, 128:]
        return carry

    lax.fori_loop(0, pieces, combine, 0)

    def m_copy(k, index):
        other = lax.rem(flat + k, R * C)
        return pltpu.make_async_remote_copy(
            src_ref=mass, dst_ref=mslots.at[index], send_sem=m_send.at[k - 1], recv_sem=m_recv.at[index],
            device_id={"rows": other // C, "cols": lax.rem(other, C)}, device_id_type=MESH,
        )

    for k in range(1, R * C):
        m_copy(k, flat).start()
    mslots[flat] = mass[...]
    for k in range(1, R * C):
        m_copy(k, lax.rem(flat + k, R * C)).wait_recv()
    total = mslots[0]
    for k in range(1, R * C):
        total = total + mslots[k]
    scale_ref[0] = jnp.sum(total)

    for k in range(1, R * C):
        m_copy(k, flat).wait_send()
    for up in (-1, 1, 0):
        for to_left in (True, False):
            cond = has_col[to_left]
            if up:
                cond = jnp.logical_and(cond, has[up])

            @pl.when(cond)
            def _():
                for copy in side(to_left, up):
                    copy.wait_send()

    def drain(p, carry):
        for up in (-1, 1):

            @pl.when(has[up])
            def _():
                for copy in rims(p, up < 0):
                    copy.wait_send()

        for k in range(1, H):
            x_copy(p, k).wait_send()
        return carry

    lax.fori_loop(0, pieces, drain, 0)


def body(mesh, hists, log_scaling_fields, histogram_weight_list):
    R, C, H = (mesh.shape[a] for a in ("rows", "cols", "hist"))
    masses, fields = hists[0], log_scaling_fields[0]
    height, width = masses.shape
    pieces = width // PIECE
    top = 2 * HALF
    dma = pltpu.SemaphoreType.DMA
    tile = jax.ShapeDtypeStruct((height, width), F32)
    any_spec = pl.BlockSpec(memory_space=pltpu.HBM)
    vmem = pl.BlockSpec(memory_space=pltpu.VMEM)
    mean, diff, scale = pl.pallas_call(
        functools.partial(kernel, (R, C, H)),
        out_shape=(tile, tile, jax.ShapeDtypeStruct((1,), F32)),
        in_specs=[pl.BlockSpec(memory_space=pltpu.SMEM), any_spec, any_spec],
        out_specs=(vmem, vmem, pl.BlockSpec(memory_space=pltpu.SMEM)),
        scratch_shapes=[
            pltpu.VMEM((pieces + 2, height + 2 * top, PIECE), F32),
            pltpu.VMEM((pieces + 2, height + top, PIECE), F32),
            pltpu.VMEM((pieces + 2, height + top, PIECE), BF16),
            pltpu.VMEM((pieces + 2, height + top, PIECE), BF16),
            pltpu.VMEM((pieces + 1, height, PIECE), BF16),
            pltpu.VMEM((pieces + 1, height, PIECE), BF16),
            pltpu.VMEM((height + top, height + 2 * top), BF16),
            pltpu.VMEM((height + top, height + 2 * top), BF16),
            pltpu.VMEM((2 * PIECE, PIECE), BF16),
            pltpu.VMEM((2 * PIECE, PIECE), BF16),
            pltpu.VMEM((pieces, height, PIECE), F32),
            pltpu.VMEM((H, pieces, height, PIECE), F32),
            pltpu.VMEM((8, 128), F32),
            pltpu.VMEM((R * C, 8, 128), F32),
            dma((4, pieces)), dma((4, pieces)),
            dma((2, 2)), dma((2, 2)),
            dma((2, 4)), dma((2, 4)),
            dma((2, pieces)),
            dma((max(H - 1, 1), pieces)), dma((H, pieces)),
            dma((max(R * C - 1, 1),)), dma((R * C,)),
        ],
        compiler_params=pltpu.CompilerParams(collective_id=0, has_side_effects=True, vmem_limit_bytes=(24 + 2 * H) << 20),
    )(histogram_weight_list, fields, masses)
    factor = float(height * R * width * C) / scale[0]
    return mean * factor, (diff + jnp.log(factor))[None]


def solution(mesh):
    return jax.shard_map(
        functools.partial(body, mesh),
        mesh=mesh,
        in_specs=(
            P("hist", ("groups", "rows"), "cols"),
            P("hist", ("groups", "rows"), "cols"),
            P(),
        ),
        out_specs=(P(("groups", "rows"), "cols"), P("hist", ("groups", "rows"), "cols")),
        check_vma=False,
    )
```

```python
import functools
import math

import jax
import jax.numpy as jnp
from jax import lax
from jax.experimental import pallas as pl
from jax.experimental.pallas import tpu as pltpu
from jax.sharding import PartitionSpec as P

HALF = 32
SIGMA = 16.0
PIECE = 256
EDGE = 128
MESH = pl.DeviceIdType.MESH
F32 = jnp.float32
BF16 = jnp.bfloat16

TAP_TOTAL = sum(math.exp(-t * t / (2.0 * SIGMA * SIGMA)) for t in range(-HALF, HALF + 1))


def split(x):
    hi = x.astype(BF16)
    lo = (x - hi.astype(F32)).astype(BF16)
    return hi, lo


def dot(a, b):
    return jnp.dot(a, b, preferred_element_type=F32)


def taps(shape, shift):
    a = lax.broadcasted_iota(jnp.int32, shape, 0)
    b = lax.broadcasted_iota(jnp.int32, shape, 1)
    t = (b - a - shift).astype(F32)
    entries = jnp.exp(-t * t / (2.0 * SIGMA * SIGMA)) / TAP_TOTAL
    return jnp.where(jnp.abs(t) <= HALF, entries, 0.0)


def kernel(
    sizes,
    w_ref, v_ref, h_ref,
    mean_ref, diff_ref, scale_ref,
    ev, eh, g1h, g1l, g3h, g3l, r1h, r1l, ch, cl, logs, slots, mass, mslots,
    z_send, z_recv, e_send, e_recv, c_send, c_recv, l_sem, x_send, x_recv, m_send, m_recv,
):
    R, C, H = sizes
    height, width = v_ref.shape
    pieces = width // PIECE
    top = 2 * HALF
    row, col, hist = lax.axis_index("rows"), lax.axis_index("cols"), lax.axis_index("hist")
    flat = row * C + col

    barrier = pltpu.get_barrier_semaphore()
    for k in range(1, R * C):
        other = lax.rem(flat + k, R * C)
        pl.semaphore_signal(
            barrier, inc=1, device_id={"rows": other // C, "cols": lax.rem(other, C)}, device_id_type=MESH
        )
    for k in range(1, H):
        pl.semaphore_signal(barrier, inc=1, device_id={"hist": lax.rem(hist + k, H)}, device_id_type=MESH)

    def own(p):
        cols = pl.ds(pl.multiple_of(p * PIECE, PIECE), PIECE)
        return (
            pltpu.make_async_copy(v_ref.at[:, cols], ev.at[p + 1, pl.ds(top, height)], l_sem.at[0, p]),
            pltpu.make_async_copy(h_ref.at[:, cols], eh.at[p + 1, pl.ds(HALF, height)], l_sem.at[1, p]),
        )

    for p in range(pieces):
        for copy in own(p):
            copy.start()

    pl.semaphore_wait(barrier, R * C - 1 + H - 1)

    def rim(src, dst, depth, edge_rows, send, recv, dev, p, to_up):
        cols = pl.ds(pl.multiple_of(p * PIECE, PIECE), PIECE)
        s = pl.ds(0, depth) if to_up else pl.ds(height - depth, depth)
        d = pl.ds(depth + height, depth) if to_up else pl.ds(0, depth)
        return pltpu.make_async_remote_copy(
            src_ref=src.at[s, cols], dst_ref=dst.at[p + 1, d], send_sem=send, recv_sem=recv,
            device_id=dev, device_id_type=MESH,
        )

    def rims(p, to_up):
        dev = {"rows": row - 1 if to_up else row + 1}
        i = 0 if to_up else 2
        return (
            rim(v_ref, ev, top, None, z_send.at[i, p], z_recv.at[i, p], dev, p, to_up),
            rim(h_ref, eh, HALF, None, z_send.at[i + 1, p], z_recv.at[i + 1, p], dev, p, to_up),
        )

    def side(to_left, up):
        out = []
        scol = pl.ds(0, EDGE) if to_left else pl.ds(width - EDGE, EDGE)
        slot = pieces + 1 if to_left else 0
        dcol = pl.ds(0, EDGE) if to_left else pl.ds(PIECE - EDGE, EDGE)
        dcolumn = col - 1 if to_left else col + 1
        for i, (src, dst, depth) in enumerate(((v_ref, ev, top), (h_ref, eh, HALF))):
            if up == 0:
                s, d = pl.ds(0, height), pl.ds(depth, height)
                dev = {"cols": dcolumn}
                a, b = e_send.at[i, int(to_left)], e_recv.at[i, int(to_left)]
            else:
                s = pl.ds(0, depth) if up < 0 else pl.ds(height - depth, depth)
                d = pl.ds(depth + height, depth) if up < 0 else pl.ds(0, depth)
                dev = {"rows": row + up, "cols": dcolumn}
                n = int(to_left) * 2 + (0 if up < 0 else 1)
                a, b = c_send.at[i, n], c_recv.at[i, n]
            out.append(
                pltpu.make_async_remote_copy(
                    src_ref=src.at[s, scol], dst_ref=dst.at[slot, d, dcol], send_sem=a, recv_sem=b,
                    device_id=dev, device_id_type=MESH,
                )
            )
        return out

    has = {-1: row > 0, 1: row < R - 1}
    has_col = {True: col > 0, False: col < C - 1}

    def send_sides(to_left):
        for up in (-1, 1, 0):
            cond = has_col[to_left]
            if up:
                cond = jnp.logical_and(cond, has[up])

            @pl.when(cond)
            def _():
                for copy in side(to_left, up):
                    copy.start()

    send_sides(False)
    for p in range(pieces):
        for up in (-1, 1):

            @pl.when(has[up])
            def _():
                for copy in rims(p, up < 0):
                    copy.start()

    send_sides(True)

    band = taps(r1h.shape, HALF)
    r1h[...], r1l[...] = split(band)
    for half in range(2):
        rows_in = lax.broadcasted_iota(jnp.int32, (PIECE, PIECE), 0) + half * PIECE
        cols_out = lax.broadcasted_iota(jnp.int32, (PIECE, PIECE), 1)
        t = (rows_in - cols_out - PIECE // 2).astype(F32)
        entries = jnp.exp(-t * t / (2.0 * SIGMA * SIGMA)) / TAP_TOTAL
        ch[half*PIECE:(half+1)*PIECE], cl[half*PIECE:(half+1)*PIECE] = split(jnp.where(jnp.abs(t) <= HALF, entries, 0.0))

    weight_sum = w_ref[0]
    for k in range(1, H):
        weight_sum = weight_sum + w_ref[k]
    own_weight = jnp.full((1, PIECE), w_ref[hist], F32) / jnp.full((1, PIECE), weight_sum, F32)

    def row_ok(rows_count, margin):
        r = lax.broadcasted_iota(jnp.int32, (rows_count, 1), 0) + (row * height - margin)
        return jnp.logical_and(r >= 0, r < R * height)

    def rows_pass(mh, ml, xh, xl):
        return dot(mh[...], xh) + dot(ml[...], xh) + dot(mh[...], xl)

    def scalings_piece(index):
        lanes = lax.broadcasted_iota(jnp.int32, (1, PIECE), 1) + (index - 1) * PIECE
        near = jnp.logical_and(lanes >= -EDGE, lanes < width + EDGE)
        g = lanes + col * width
        ok_cols = jnp.logical_and(near, jnp.logical_and(g >= 0, g < C * width))
        ok = jnp.logical_and(row_ok(height + 2 * top, top), ok_cols)
        f = jnp.where(ok, jnp.exp(ev[index]), 0.0)
        fh, fl = split(f)
        g1h[index], g1l[index] = split(rows_pass(r1h, r1l, fh, fl))

    def cols_pass(ah, al, j):
        xh = jnp.concatenate([ah[j], ah[j + 1]], axis=1)
        xl = jnp.concatenate([al[j], al[j + 1]], axis=1)
        total = dot(xh, ch[...]) + dot(xl, ch[...]) + dot(xh, cl[...])
        return total

    def arrive(conds, make):
        cond = conds[0]
        for c in conds[1:]:
            cond = jnp.logical_and(cond, c)

        @pl.when(cond)
        def _():
            for copy in make():
                copy.wait_recv()

    def wait_side(to_left):
        came = has_col[not to_left]
        arrive((came,), lambda: side(to_left, 0))
        for up in (-1, 1):
            arrive((came, has[-up]), lambda: side(to_left, up))

    wait_side(False)
    scalings_piece(0)

    def x_copy(c, k):
        other = lax.rem(hist + k, H)
        return pltpu.make_async_remote_copy(
            src_ref=slots.at[hist, c], dst_ref=slots.at[hist, c],
            send_sem=x_send.at[k - 1, c], recv_sem=x_recv.at[hist, c],
            device_id={"hist": other}, device_id_type=MESH,
        )

    def step(j, carry):
        @pl.when(j < pieces)
        def _():
            for copy in own(j):
                copy.wait()
            for up in (-1, 1):
                arrive((has[-up],), lambda: rims(j, up < 0))

        @pl.when(j == pieces)
        def _():
            wait_side(True)

        scalings_piece(j + 1)
        smooth_v = cols_pass(g1h, g1l, j)
        masses = jnp.concatenate([eh[j, :, PIECE // 2 :], eh[j + 1, :, : PIECE // 2]], axis=1)
        lanes = lax.broadcasted_iota(jnp.int32, (1, PIECE), 1) + (j * PIECE - PIECE // 2 + col * width)
        ok = jnp.logical_and(
            row_ok(height + top, HALF), jnp.logical_and(lanes >= 0, lanes < C * width)
        )
        ratios = jnp.where(ok, masses / smooth_v, 0.0)
        fill = jnp.zeros((top, PIECE), F32)
        rh, rl = split(jnp.concatenate([ratios, fill], axis=0))
        g3h[j], g3l[j] = split(rows_pass(r1h.at[pl.ds(0, height)], r1l.at[pl.ds(0, height)], rh, rl))

        @pl.when(j >= 1)
        def _():
            c = j - 1
            log_smooth = jnp.log(cols_pass(g3h, g3l, c))
            logs[c] = log_smooth
            slots[hist, c] = own_weight * (ev[c + 1, pl.ds(top, height)] + log_smooth)
            for k in range(1, H):
                x_copy(c, k).start()

        return carry

    for j in range(pieces + 1):
        step(j, 0)

    mass[...] = jnp.zeros_like(mass)

    def combine(c, carry):
        for k in range(1, H):
            source = lax.rem(hist + k, H)
            pltpu.make_async_remote_copy(
                src_ref=slots.at[source, c], dst_ref=slots.at[source, c],
                send_sem=x_send.at[k - 1, c], recv_sem=x_recv.at[source, c],
                device_id={"hist": source}, device_id_type=MESH,
            ).wait_recv()
        log_mean = slots[0, c]
        for k in range(1, H):
            log_mean = log_mean + slots[k, c]
        mean = jnp.exp(log_mean)
        cols = pl.ds(pl.multiple_of(c * PIECE, PIECE), PIECE)
        mean_ref[:, cols] = mean
        diff_ref[:, cols] = log_mean - logs[c]
        part = jnp.sum(mean.reshape(height // 8, 8, PIECE), axis=0)
        mass[...] += part[:, :128] + part[:, 128:]
        return carry

    lax.fori_loop(0, pieces, combine, 0)

    def m_copy(k, index):
        other = lax.rem(flat + k, R * C)
        return pltpu.make_async_remote_copy(
            src_ref=mass, dst_ref=mslots.at[index], send_sem=m_send.at[k - 1], recv_sem=m_recv.at[index],
            device_id={"rows": other // C, "cols": lax.rem(other, C)}, device_id_type=MESH,
        )

    for k in range(1, R * C):
        m_copy(k, flat).start()
    mslots[flat] = mass[...]
    for k in range(1, R * C):
        m_copy(k, lax.rem(flat + k, R * C)).wait_recv()
    total = mslots[0]
    for k in range(1, R * C):
        total = total + mslots[k]
    scale_ref[0] = jnp.sum(total)

    for k in range(1, R * C):
        m_copy(k, flat).wait_send()
    for up in (-1, 1, 0):
        for to_left in (True, False):
            cond = has_col[to_left]
            if up:
                cond = jnp.logical_and(cond, has[up])

            @pl.when(cond)
            def _():
                for copy in side(to_left, up):
                    copy.wait_send()

    def drain(p, carry):
        for up in (-1, 1):

            @pl.when(has[up])
            def _():
                for copy in rims(p, up < 0):
                    copy.wait_send()

        for k in range(1, H):
            x_copy(p, k).wait_send()
        return carry

    lax.fori_loop(0, pieces, drain, 0)


def body(mesh, hists, log_scaling_fields, histogram_weight_list):
    R, C, H = (mesh.shape[a] for a in ("rows", "cols", "hist"))
    masses, fields = hists[0], log_scaling_fields[0]
    height, width = masses.shape
    pieces = width // PIECE
    top = 2 * HALF
    dma = pltpu.SemaphoreType.DMA
    tile = jax.ShapeDtypeStruct((height, width), F32)
    any_spec = pl.BlockSpec(memory_space=pltpu.HBM)
    vmem = pl.BlockSpec(memory_space=pltpu.VMEM)
    mean, diff, scale = pl.pallas_call(
        functools.partial(kernel, (R, C, H)),
        out_shape=(tile, tile, jax.ShapeDtypeStruct((1,), F32)),
        in_specs=[pl.BlockSpec(memory_space=pltpu.SMEM), any_spec, any_spec],
        out_specs=(vmem, vmem, pl.BlockSpec(memory_space=pltpu.SMEM)),
        scratch_shapes=[
            pltpu.VMEM((pieces + 2, height + 2 * top, PIECE), F32),
            pltpu.VMEM((pieces + 2, height + top, PIECE), F32),
            pltpu.VMEM((pieces + 2, height + top, PIECE), BF16),
            pltpu.VMEM((pieces + 2, height + top, PIECE), BF16),
            pltpu.VMEM((pieces + 1, height, PIECE), BF16),
            pltpu.VMEM((pieces + 1, height, PIECE), BF16),
            pltpu.VMEM((height + top, height + 2 * top), BF16),
            pltpu.VMEM((height + top, height + 2 * top), BF16),
            pltpu.VMEM((2 * PIECE, PIECE), BF16),
            pltpu.VMEM((2 * PIECE, PIECE), BF16),
            pltpu.VMEM((pieces, height, PIECE), F32),
            pltpu.VMEM((H, pieces, height, PIECE), F32),
            pltpu.VMEM((8, 128), F32),
            pltpu.VMEM((R * C, 8, 128), F32),
            dma((4, pieces)), dma((4, pieces)),
            dma((2, 2)), dma((2, 2)),
            dma((2, 4)), dma((2, 4)),
            dma((2, pieces)),
            dma((max(H - 1, 1), pieces)), dma((H, pieces)),
            dma((max(R * C - 1, 1),)), dma((R * C,)),
        ],
        compiler_params=pltpu.CompilerParams(collective_id=0, has_side_effects=True, vmem_limit_bytes=51 << 20),
    )(histogram_weight_list, fields, masses)
    factor = float(height * R * width * C) / scale[0]
    return mean * factor, (diff + jnp.log(factor))[None]


def solution(mesh):
    return jax.shard_map(
        functools.partial(body, mesh),
        mesh=mesh,
        in_specs=(
            P("hist", ("groups", "rows"), "cols"),
            P("hist", ("groups", "rows"), "cols"),
            P(),
        ),
        out_specs=(P(("groups", "rows"), "cols"), P("hist", ("groups", "rows"), "cols")),
        check_vma=False,
    )
```
